128 devices in a mesh: expert: 32 (over z, x, core), shard: 4 (over y).
Axes of the slice: x: 4, y: 4, z: 4, core: 2. Of those that a mesh axis runs over, the one named last changes fastest.
Arguments:
- tokens: bfloat16 [32768, 1024], P(('expert', 'shard')), may hold values from -6 to 6
- segments: int32 [32, 1024], P('expert', 'shard'), may hold values from 0 to 3, never falling along the last dimension, each value on 1 to 768 neighbouring positions
- expert_ids: int32 [32768, 8], P(('expert', 'shard')), may hold values from 0 to 31, all different within a row; in each aligned block of 256 rows (0 to 255, 256 to 511, ...) at most 72 rows name the same one
- attn_norm: bfloat16 [1024], P('shard'), may hold values from 0.5 to 1.5
- query_weight: bfloat16 [1024, 1024], P('shard'), may hold values from -0.1875 to 0.1875
- key_matrix: bfloat16 [1024, 512], P('shard'), may hold values from -0.1875 to 0.1875
- value_matrix: bfloat16 [1024, 512], P('shard'), may hold values from -0.1875 to 0.1875
- output_weight: bfloat16 [1024, 1024], P(None, 'shard'), may hold values from -1.5 to 1.5
- ffn_norm: bfloat16 [1024], P('shard'), may hold values from 0.5 to 1.5
- router_weight: bfloat16 [1024, 32], P('shard'), may hold values from -0.1875 to 0.1875
- gate_weight: bfloat16 [32, 1024, 512], P('expert', 'shard'), may hold values from -0.1875 to 0.1875
- up_weight: bfloat16 [32, 1024, 512], P('expert', 'shard'), may hold values from -0.1875 to 0.1875
- down_weight: bfloat16 [32, 512, 1024], P('expert', None, 'shard'), may hold values from -0.75 to 0.75
- cotangent: bfloat16 [32768, 1024], P(('expert', 'shard')), may hold values from -24 to 24
Outputs:
- output: bfloat16 [32768, 1024], P(('expert', 'shard'))
- d_tokens: bfloat16 [32768, 1024], P(('expert', 'shard'))
- d_attn_norm: float32 [1024], P('shard')
- d_query: float32 [1024, 1024], P('shard')
- d_key: float32 [1024, 512], P('shard')
- d_value: float32 [1024, 512], P('shard')
- d_output_weight: float32 [1024, 1024], P(None, 'shard')
- d_ffn_norm: float32 [1024], P('shard')
- d_router: float32 [1024, 32], P('shard')
- d_gate: float32 [32, 1024, 512], P('expert', 'shard')
- d_up: float32 [32, 1024, 512], P('expert', 'shard')
- d_down: float32 [32, 512, 1024], P('expert', None, 'shard')
The draws below stay inside these ranges and needn't reach their ends.
Inputs may be any that keep to these rules, and one draw needn't show every extreme that they name: `expert_ids`: each row names 8 different experts. Among the 256 rows of one device no expert is named more than 72 times, a bound that some block reaches. `segments`: along each sequence the numbers never fall; each document has 1 to 768 tokens, and one has exactly 768.
All inputs are finite; a program needn't handle non-finite values.
Results may differ from the reference program's by a relative error of at most 0.025.
Values may be sent and summed in bfloat16 or wider, within the bound.
A program may use at most 192 MiB of HBM per device.

```python
import math
import jax
import jax.numpy as jnp
import numpy as np
from jax import lax

MODEL_WIDTH = 1024
QUERY_HEADS = 16
KEY_VALUE_HEADS = 8
HEAD_SIZE = 64
FF = 512
TOPK = 8
SEG_COUNT = 4
TOK_DEV = 256
EXPERTS = 32
SEQUENCE_LENGTH = 1024
NSEQ = 32
TOKENS = 32768
CAP = 72
DOC_MOST = 768
N_EXPERT = 32
N_SHARD = 4


def strengthened(values, rng, source, target, blocks, factor):
    def block_of(position):
        return (jnp.arange(values.shape[position]) // (values.shape[position] // blocks)).reshape((-1,) + (1,) * (values.ndim - 1 - position))

    near = jax.random.permutation(rng, blocks)[block_of(target)]
    other_side = (block_of(target) + blocks // 2) % blocks
    return jnp.where((block_of(source) == near) | (block_of(source) == other_side), factor * values, values)


def levels(stream_key, extent, pieces, smallest, top_value):
    def one(dim, shards_of):
        draws = jax.random.uniform(jax.random.fold_in(jax.random.fold_in(stream_key, 6), dim), (shards_of,), jnp.float32, smallest / len(pieces), top_value / len(pieces))
        return jnp.repeat(jnp.exp(draws), extent[dim] // shards_of).reshape((-1,) + (1,) * (len(extent) - dim - 1))

    loudness = one(*pieces[0])
    for cut in pieces[1:]:
        loudness = loudness * one(*cut)
    return loudness


def profile(count, total, bound, lean):
    loads = [(1 << 20) // math.isqrt(standing ** lean) + 1 for standing in range(2, count + 1)]
    rest, holding = total - bound - (count - 1), [1] * (count - 1)
    while rest > 0:
        candidates = [i for i in range(count - 1) if holding[i] < bound]
        whole, remaining = sum([loads[i] for i in candidates]), rest
        for i in candidates:
            more = min(bound - holding[i], max(1, remaining * loads[i] // whole), rest)
            holding[i] = holding[i] + more
            rest = rest - more
    return np.array([bound] + holding)


def ragged(rng, number_of, total, limit, slope):
    if number_of == 2:
        one = jax.random.randint(rng, (), max(1, total - limit), min(limit, total - 1) + 1)
        return jnp.stack([one, total - one])
    tallies = jnp.asarray(profile(number_of, total, limit, slope), jnp.int32)
    couples = (number_of - 1) // 2
    donor, receiver = tallies[1:1 + 2 * couples:2], tallies[2:2 + 2 * couples:2]
    margin = jnp.minimum(donor - 1, limit - receiver)
    moved = jax.random.randint(jax.random.fold_in(rng, 1), (couples,), 0, 1 << 20) % (margin + 1)
    tallies = tallies.at[1:1 + 2 * couples:2].set(donor - moved).at[2:2 + 2 * couples:2].set(receiver + moved)
    return tallies[jax.random.permutation(jax.random.fold_in(rng, 2), number_of)]


def routed_block(stream_key, own, number, rows, amount, top, most, lean):
    ranking = jax.random.permutation(stream_key, amount)
    crowded, usual = portions_of(amount, rows * top, most, lean, True), portions_of(amount, rows * top, most, lean, False)
    places = jnp.arange(amount)

    def named(lengths, offset_by):
        used = int((lengths > 0).sum())
        fixed = max(1, used // 4)
        passed = fixed + (places - fixed + offset_by * (used - fixed)) % max(1, amount - fixed)
        return jnp.zeros((amount,), jnp.int32).at[ranking[jnp.where(places < fixed, places, passed)]].set(jnp.asarray(lengths, jnp.int32))

    lengths = jnp.where(number % 4 == 0, named(crowded, number // 4), named(usual, number - number // 4 - 1))
    mixed = jax.random.permutation(jax.random.fold_in(own, 3), amount)
    source_of, taker = mixed[0:amount // 2 * 2:2], mixed[1:amount // 2 * 2:2]
    room = jnp.minimum(lengths[source_of] - 1, most - lengths[taker]) // 2
    room = jnp.where((source_of == ranking[0]) | (taker == ranking[0]) | (lengths[taker] == 0), 0, jnp.maximum(room, 0))
    passed = jax.random.randint(jax.random.fold_in(own, 4), (amount // 2,), 0, 1 << 20) % (room + 1)
    lengths = lengths.at[source_of].add(-passed).at[taker].add(passed)
    items = jnp.searchsorted(jnp.cumsum(lengths), jnp.arange(rows * top), side="right").astype(jnp.int32)
    listing = items.reshape(top, rows).T
    listing = listing[jax.random.permutation(jax.random.fold_in(own, 1), rows)]
    offset_by = jax.random.randint(jax.random.fold_in(own, 2), (rows, 1), 0, top)
    return jnp.take_along_axis(listing, (jnp.arange(top)[None, :] + offset_by) % top, axis=1)


def portions_of(number_of, total, bound, slope, full):
    loads = [(1 << 20) // math.isqrt(grade ** slope) + 1 for grade in range(1, number_of + 1)]
    largest = bound if full else min(bound, max(-(-total // number_of), total * loads[0] // sum(loads)))
    least = 1 if total - largest >= number_of - 1 else 0
    counts, spare = [largest] + [least] * (number_of - 1), total - largest - least * (number_of - 1)
    while spare > 0:
        candidates = [i for i in range(1, number_of) if counts[i] < largest] or [i for i in range(1, number_of) if counts[i] < bound]
        pool, remaining = sum([loads[i] for i in candidates]), spare
        for i in candidates:
            extra = min(bound - counts[i], max(1, remaining * loads[i] // pool), spare)
            counts[i] = counts[i] + extra
            spare = spare - extra
    return np.array(counts)


def scatter_about(stream_key, dims, width, most, cuts=(), held_as=jnp.bfloat16):
    array = width * jax.random.normal(stream_key, dims, jnp.float32)
    if cuts:
        array = array * levels(stream_key, dims, cuts, -0.22, 0.18)
    return jnp.clip(array, -most, most).astype(held_as)


def bell_draw_with(own_key, dims, deviation, reach, pieces, heavy, kind=jnp.bfloat16):
    values = deviation * jax.random.normal(own_key, dims, jnp.float32)
    if pieces:
        values = values * levels(own_key, dims, pieces, -0.22, 0.18)
    return jnp.clip(strengthened(values, jax.random.fold_in(own_key, 3), *heavy), -reach, reach).astype(kind)


def setup_inputs(seed: int = 0) -> dict:
    streams_of = jax.random.split(jax.random.key(seed), 15)
    tokens = scatter_about(streams_of[0], (TOKENS, MODEL_WIDTH), 1.0, 6.0, ((0, 128),))
    segments = jax.vmap(lambda own: jnp.searchsorted(jnp.cumsum(ragged(own, SEG_COUNT, SEQUENCE_LENGTH, DOC_MOST, 1)), jnp.arange(SEQUENCE_LENGTH), side="right"))(jax.random.split(streams_of[1], NSEQ)).reshape((NSEQ, SEQUENCE_LENGTH)).astype(jnp.int32)
    expert_ids_keys = jax.random.split(jax.random.fold_in(streams_of[2], 1), TOKENS // TOK_DEV)
    expert_ids_turns = jax.random.permutation(jax.random.fold_in(streams_of[2], 3), TOKENS // TOK_DEV)
    expert_ids = jax.vmap(lambda own, number: routed_block(jax.random.fold_in(streams_of[2], 2), own, number, TOK_DEV, EXPERTS, TOPK, CAP, 2))(expert_ids_keys, expert_ids_turns).reshape((TOKENS, TOPK))
    attn_norm = jnp.clip(1.0 + 0.1 * jax.random.normal(streams_of[3], (MODEL_WIDTH,), jnp.float32), 0.5, 1.5).astype(jnp.bfloat16)
    query_weight = scatter_about(streams_of[4], (MODEL_WIDTH, QUERY_HEADS * HEAD_SIZE), MODEL_WIDTH ** -0.5, 0.1875, ((0, 4),))
    key_matrix = scatter_about(streams_of[5], (MODEL_WIDTH, KEY_VALUE_HEADS * HEAD_SIZE), MODEL_WIDTH ** -0.5, 0.1875, ((0, 4),))
    value_matrix = scatter_about(streams_of[6], (MODEL_WIDTH, KEY_VALUE_HEADS * HEAD_SIZE), MODEL_WIDTH ** -0.5, 0.1875, ((0, 4),))
    output_weight = scatter_about(streams_of[7], (QUERY_HEADS * HEAD_SIZE, MODEL_WIDTH), (QUERY_HEADS * HEAD_SIZE // 64) ** -0.5, 1.5, ((1, 4),))
    ffn_norm = jnp.clip(1.0 + 0.1 * jax.random.normal(streams_of[8], (MODEL_WIDTH,), jnp.float32), 0.5, 1.5).astype(jnp.bfloat16)
    router_weight = scatter_about(streams_of[9], (MODEL_WIDTH, EXPERTS), MODEL_WIDTH ** -0.5, 0.1875, ((0, 4),))
    gate_weight = scatter_about(streams_of[10], (EXPERTS, MODEL_WIDTH, FF), MODEL_WIDTH ** -0.5, 0.1875, ((0, 32), (1, 4)))
    up_weight = scatter_about(streams_of[11], (EXPERTS, MODEL_WIDTH, FF), MODEL_WIDTH ** -0.5, 0.1875, ((0, 32), (1, 4)))
    down_weight = scatter_about(streams_of[12], (EXPERTS, FF, MODEL_WIDTH), (FF // 8) ** -0.5, 0.75, ((0, 32), (2, 4)))
    cotangent = bell_draw_with(streams_of[13], (TOKENS, MODEL_WIDTH), 1.0, 24.0, ((0, 128),), (0, 1, 128, 5.5))
    return {"tokens": tokens, "segments": segments, "expert_ids": expert_ids, "attn_norm": attn_norm, "query_weight": query_weight, "key_matrix": key_matrix, "value_matrix": value_matrix, "output_weight": output_weight, "ffn_norm": ffn_norm, "router_weight": router_weight, "gate_weight": gate_weight, "up_weight": up_weight, "down_weight": down_weight, "cotangent": cotangent}


EPS = 1e-05
BASE = 10000.0

def rms_scale(values):
    return lax.rsqrt(lax.optimization_barrier(jnp.mean(values * values, axis=-1, keepdims=True)) + EPS)

def rope_tables(length):
    half_dim = HEAD_SIZE // 2
    inverse = BASE ** (-jnp.arange(half_dim, dtype=jnp.float32) * 2.0 / HEAD_SIZE)
    angles = jnp.arange(length, dtype=jnp.float32)[:, None] * inverse[None, :]
    return (jnp.cos(angles)[:, None, :], jnp.sin(angles)[:, None, :])

def apply_rotary(values, cosine_table, sine_table):
    half_dim = values.shape[-1] // 2
    first_half = values[..., :half_dim]
    second_half = values[..., half_dim:]
    return jnp.concatenate([first_half * cosine_table - second_half * sine_table, second_half * cosine_table + first_half * sine_table], axis=-1)

def reverse_rotary(grads, cosine_table, sine_table):
    half_dim = grads.shape[-1] // 2
    first_half = grads[..., :half_dim]
    second_half = grads[..., half_dim:]
    return jnp.concatenate([first_half * cosine_table + second_half * sine_table, second_half * cosine_table - first_half * sine_table], axis=-1)

def reference(tokens, segments, expert_ids, attn_norm, query_weight, key_matrix, value_matrix, output_weight, ffn_norm, router_weight, gate_weight, up_weight, down_weight, cotangent):
    single_float = jnp.float32
    brain_float_half = jnp.bfloat16
    query_group_width = QUERY_HEADS // KEY_VALUE_HEADS
    score_scale = HEAD_SIZE ** (-0.5)
    cosine_table, sine_table = rope_tables(SEQUENCE_LENGTH)
    positions = jnp.arange(SEQUENCE_LENGTH, dtype=jnp.int32)
    causal = positions[None, :] <= positions[:, None]
    gain_one = attn_norm.astype(single_float)
    gain_two = ffn_norm.astype(single_float)

    def score_table(query_rotated, key_rotated, seg_seq):
        query_by_group = query_rotated.astype(single_float).reshape(SEQUENCE_LENGTH, KEY_VALUE_HEADS, query_group_width, HEAD_SIZE)
        key_head_rows = key_rotated.astype(single_float).reshape(SEQUENCE_LENGTH, KEY_VALUE_HEADS, HEAD_SIZE)
        scores = jnp.einsum('tgrd,sgd->tgrs', query_by_group, key_head_rows) * score_scale
        allowed = causal & (seg_seq[None, :] == seg_seq[:, None])
        return (scores, allowed[:, None, None, :])

    def attend_forward(totals, inputs):
        x_seq, seg_seq = inputs
        x_float = x_seq.astype(single_float)
        scale_one = rms_scale(x_float)
        hidden_first = (x_float * scale_one * gain_one).astype(brain_float_half)
        query_rotated = apply_rotary(jnp.dot(hidden_first, query_weight, preferred_element_type=single_float).reshape(SEQUENCE_LENGTH, QUERY_HEADS, HEAD_SIZE), cosine_table, sine_table).astype(brain_float_half)
        key_rotated = apply_rotary(jnp.dot(hidden_first, key_matrix, preferred_element_type=single_float).reshape(SEQUENCE_LENGTH, KEY_VALUE_HEADS, HEAD_SIZE), cosine_table, sine_table).astype(brain_float_half)
        value_row_block = jnp.dot(hidden_first, value_matrix, preferred_element_type=single_float).astype(brain_float_half)
        scores, allowed = score_table(query_rotated, key_rotated, seg_seq)
        exponent = jnp.where(allowed, jnp.exp(scores), 0.0)
        log_total = jnp.log(lax.optimization_barrier(jnp.sum(exponent, axis=-1)))
        attention_probs = jnp.where(allowed, jnp.exp(scores - log_total[..., None]), 0.0).astype(brain_float_half)
        attended_rows = jnp.einsum('qaim,mal->qail', attention_probs.astype(single_float), value_row_block.astype(single_float).reshape(SEQUENCE_LENGTH, KEY_VALUE_HEADS, HEAD_SIZE)).astype(brain_float_half).reshape(SEQUENCE_LENGTH, QUERY_HEADS * HEAD_SIZE)
        resid = x_float + jnp.dot(attended_rows, output_weight, preferred_element_type=single_float)
        scale_two = rms_scale(resid)
        hidden_two = (resid * scale_two * gain_two).astype(brain_float_half)
        return (totals, (hidden_first, query_rotated, key_rotated, value_row_block, log_total, attended_rows, resid, hidden_two))
    seq_tokens = tokens.reshape(NSEQ, SEQUENCE_LENGTH, MODEL_WIDTH)
    unused, kept = lax.scan(attend_forward, jnp.zeros((), single_float), (seq_tokens, segments))
    hidden_one_all, query_all, key_all, value_all, log_all, attended_all, resid_seq, hidden_seq = kept
    resid = resid_seq.reshape(TOKENS, MODEL_WIDTH)
    hidden_two = hidden_seq.reshape(TOKENS, MODEL_WIDTH)
    logits = jnp.dot(hidden_two, router_weight, preferred_element_type=single_float)
    chosen = jnp.take_along_axis(logits, expert_ids, axis=1)
    gate_exp = jnp.exp(chosen)
    gates = gate_exp / lax.optimization_barrier(jnp.sum(gate_exp, axis=-1, keepdims=True))
    flat_ids = expert_ids.reshape(-1)
    gates_flat = gates.reshape(-1)
    cot_float = cotangent.astype(single_float)
    row_limit = min(TOKENS, CAP * N_EXPERT * N_SHARD)

    def expert_step(totals, inputs):
        combined, d_gates_flat, d_hidden_moe = totals
        expert, w_gate, w_up, w_down = inputs
        member = flat_ids == expert
        row_count = jnp.sum(member.astype(jnp.int32))
        slot_index, = jnp.nonzero(member, size=row_limit, fill_value=0)
        slot_index = slot_index.astype(jnp.int32)
        usable = jnp.arange(row_limit, dtype=jnp.int32) < row_count
        owners = slot_index // TOPK
        rows_in = hidden_two[owners]
        weight_slot = jnp.where(usable, gates_flat[slot_index], 0.0)
        gate_pre = jnp.dot(rows_in, w_gate, preferred_element_type=single_float)
        up_pre = jnp.dot(rows_in, w_up, preferred_element_type=single_float)
        sigmoid_pre = jax.nn.sigmoid(gate_pre)
        activ = gate_pre * sigmoid_pre
        mid = (activ * up_pre).astype(brain_float_half)
        result = jnp.dot(mid, w_down, preferred_element_type=single_float).astype(brain_float_half)
        result_float = result.astype(single_float)
        combined = combined.at[owners].add(weight_slot[:, None] * result_float)
        cot_rows = cot_float[owners]
        d_gate_slot = jnp.where(usable, lax.optimization_barrier(jnp.sum(cot_rows * result_float, axis=-1)), 0.0)
        d_gates_flat = d_gates_flat.at[slot_index].add(d_gate_slot)
        d_result = (weight_slot[:, None] * cot_rows).astype(brain_float_half)
        d_mid = jnp.dot(d_result, w_down.T, preferred_element_type=single_float)
        grad_down = jnp.dot(mid.T, d_result, preferred_element_type=single_float)
        d_gate_pre = (d_mid * up_pre * sigmoid_pre * (1.0 + gate_pre * (1.0 - sigmoid_pre))).astype(brain_float_half)
        d_up_pre = (d_mid * activ).astype(brain_float_half)
        grad_gate = jnp.dot(rows_in.T, d_gate_pre, preferred_element_type=single_float)
        grad_up = jnp.dot(rows_in.T, d_up_pre, preferred_element_type=single_float)
        d_rows = (jnp.dot(d_gate_pre, w_gate.T, preferred_element_type=single_float) + jnp.dot(d_up_pre, w_up.T, preferred_element_type=single_float)).astype(brain_float_half)
        d_hidden_moe = d_hidden_moe.at[owners].add(d_rows.astype(single_float))
        return ((combined, d_gates_flat, d_hidden_moe), (grad_gate, grad_up, grad_down))
    start = (jnp.zeros((TOKENS, MODEL_WIDTH), single_float), jnp.zeros((TOKENS * TOPK,), single_float), jnp.zeros((TOKENS, MODEL_WIDTH), single_float))
    ends, expert_grads = lax.scan(expert_step, start, (jnp.arange(EXPERTS, dtype=jnp.int32), gate_weight, up_weight, down_weight))
    combined, d_gates_flat, d_hidden_moe = ends
    d_gate, d_up, d_down = expert_grads
    output = (resid + combined).astype(brain_float_half)
    d_gates = d_gates_flat.reshape(TOKENS, TOPK)
    d_chosen = gates * (d_gates - lax.optimization_barrier(jnp.sum(gates * d_gates, axis=-1, keepdims=True)))
    onehot = (expert_ids[:, :, None] == jnp.arange(EXPERTS, dtype=jnp.int32)[None, None, :]).astype(single_float)
    d_logits = lax.optimization_barrier(jnp.sum(onehot * d_chosen[:, :, None], axis=1)).astype(brain_float_half)
    d_router = jnp.dot(hidden_two.T, d_logits, preferred_element_type=single_float)
    d_hidden_two = d_hidden_moe + jnp.dot(d_logits, router_weight.T, preferred_element_type=single_float)
    scale_two = rms_scale(resid)
    normed_two = resid * scale_two
    d_ffn_norm = lax.optimization_barrier(jnp.sum(d_hidden_two * normed_two, axis=0))
    m_two = d_hidden_two * gain_two
    d_resid = cot_float + scale_two * (m_two - normed_two * lax.optimization_barrier(jnp.mean(m_two * normed_two, axis=-1, keepdims=True)))

    def attend_backward(totals, inputs):
        grad_query, grad_key, grad_value, grad_output, grad_norm = totals
        x_seq, seg_seq, hidden_first, query_rotated, key_rotated, value_row_block, log_total, attended_rows, d_resid_seq = inputs
        d_attn = d_resid_seq.astype(brain_float_half)
        grad_output = grad_output + jnp.dot(attended_rows.T, d_attn, preferred_element_type=single_float)
        grad_attended = jnp.dot(d_attn, output_weight.T, preferred_element_type=single_float).astype(brain_float_half)
        scores, allowed = score_table(query_rotated, key_rotated, seg_seq)
        probs_full = jnp.where(allowed, jnp.exp(scores - log_total[..., None]), 0.0)
        probs_round = probs_full.astype(brain_float_half).astype(single_float)
        grad_attended_four = grad_attended.astype(single_float).reshape(SEQUENCE_LENGTH, KEY_VALUE_HEADS, query_group_width, HEAD_SIZE)
        value_head_rows = value_row_block.astype(single_float).reshape(SEQUENCE_LENGTH, KEY_VALUE_HEADS, HEAD_SIZE)
        grad_values = jnp.einsum('qkaz,qkay->zky', probs_round, grad_attended_four)
        d_probs = jnp.einsum('tgrd,sgd->tgrs', grad_attended_four, value_head_rows)
        softmax_correction = lax.optimization_barrier(jnp.sum(grad_attended_four * attended_rows.astype(single_float).reshape(SEQUENCE_LENGTH, KEY_VALUE_HEADS, query_group_width, HEAD_SIZE), axis=-1))
        grad_scores = (probs_full * (d_probs - softmax_correction[..., None]) * score_scale).astype(brain_float_half).astype(single_float)
        grad_query_unrotated = jnp.einsum('qaim,mal->qail', grad_scores, key_rotated.astype(single_float).reshape(SEQUENCE_LENGTH, KEY_VALUE_HEADS, HEAD_SIZE))
        grad_key_unrotated = jnp.einsum('qkaz,qkay->zky', grad_scores, query_rotated.astype(single_float).reshape(SEQUENCE_LENGTH, KEY_VALUE_HEADS, query_group_width, HEAD_SIZE))
        dq_rows = reverse_rotary(grad_query_unrotated.reshape(SEQUENCE_LENGTH, QUERY_HEADS, HEAD_SIZE), cosine_table, sine_table).astype(brain_float_half).reshape(SEQUENCE_LENGTH, QUERY_HEADS * HEAD_SIZE)
        grad_key_rows = reverse_rotary(grad_key_unrotated, cosine_table, sine_table).astype(brain_float_half).reshape(SEQUENCE_LENGTH, KEY_VALUE_HEADS * HEAD_SIZE)
        grad_value_rows = grad_values.reshape(SEQUENCE_LENGTH, KEY_VALUE_HEADS * HEAD_SIZE).astype(brain_float_half)
        grad_query = grad_query + jnp.dot(hidden_first.T, dq_rows, preferred_element_type=single_float)
        grad_key = grad_key + jnp.dot(hidden_first.T, grad_key_rows, preferred_element_type=single_float)
        grad_value = grad_value + jnp.dot(hidden_first.T, grad_value_rows, preferred_element_type=single_float)
        d_hidden_one = jnp.dot(dq_rows, query_weight.T, preferred_element_type=single_float) + jnp.dot(grad_key_rows, key_matrix.T, preferred_element_type=single_float) + jnp.dot(grad_value_rows, value_matrix.T, preferred_element_type=single_float)
        x_float = x_seq.astype(single_float)
        scale_one = rms_scale(x_float)
        normed_one = x_float * scale_one
        grad_norm = grad_norm + lax.optimization_barrier(jnp.sum(d_hidden_one * normed_one, axis=0))
        m_one = d_hidden_one * gain_one
        d_x = d_resid_seq + scale_one * (m_one - normed_one * lax.optimization_barrier(jnp.mean(m_one * normed_one, axis=-1, keepdims=True)))
        return ((grad_query, grad_key, grad_value, grad_output, grad_norm), d_x.astype(brain_float_half))
    start_backward = (jnp.zeros((MODEL_WIDTH, QUERY_HEADS * HEAD_SIZE), single_float), jnp.zeros((MODEL_WIDTH, KEY_VALUE_HEADS * HEAD_SIZE), single_float), jnp.zeros((MODEL_WIDTH, KEY_VALUE_HEADS * HEAD_SIZE), single_float), jnp.zeros((QUERY_HEADS * HEAD_SIZE, MODEL_WIDTH), single_float), jnp.zeros((MODEL_WIDTH,), single_float))
    grads_back, d_tokens_seq = lax.scan(attend_backward, start_backward, (seq_tokens, segments, hidden_one_all, query_all, key_all, value_all, log_all, attended_all, d_resid.reshape(NSEQ, SEQUENCE_LENGTH, MODEL_WIDTH)))
    d_query, d_key, d_value, d_output_weight, d_attn_norm = grads_back
    d_tokens = d_tokens_seq.reshape(TOKENS, MODEL_WIDTH)
    return (output, d_tokens, d_attn_norm, d_query, d_key, d_value, d_output_weight, d_ffn_norm, d_router, d_gate, d_up, d_down)
```

```python
import functools

import jax
import jax.numpy as jnp
from jax import lax
from jax.experimental import pallas as pl
from jax.experimental.pallas import tpu as pltpu
from jax.sharding import PartitionSpec as P

D = 1024
NH = 16
NKV = 8
HD = 64
FF = 512
TOPK = 8
NE = 32
NS = 4
T = 256
CAP = 72
SLOTS = NE * CAP
GC = 512
EPS = 1e-05
BASE = 10000.0
F32 = jnp.float32
BF = jnp.bfloat16
MESH = pl.DeviceIdType.MESH
ANY = pl.BlockSpec(memory_space=pl.ANY)
VM = pl.BlockSpec(memory_space=pltpu.VMEM)
DMA = pltpu.SemaphoreType.DMA
SMALL = 64


def nn(a, b):
    return lax.dot_general(a, b, (((1,), (0,)), ((), ())), preferred_element_type=F32)


def nt(a, b):
    return lax.dot_general(a, b, (((1,), (1,)), ((), ())), preferred_element_type=F32)


def tn(a, b):
    return lax.dot_general(a, b, (((0,), (0,)), ((), ())), preferred_element_type=F32)


def sds(shape, dtype):
    return jax.ShapeDtypeStruct(shape, dtype)


def plain(kernel, outs, *args, name, flops=0, moved=0, **kw):
    return pl.pallas_call(
        kernel,
        out_shape=outs,
        in_specs=[VM] * len(args),
        out_specs=jax.tree.map(lambda _: VM, outs),
        compiler_params=pltpu.CompilerParams(vmem_limit_bytes=56 << 20),
        cost_estimate=pl.CostEstimate(flops=flops, bytes_accessed=moved, transcendentals=0),
        name=name,
        **kw,
    )(*args)


def gather_front_kernel(x, wq, wk, wv, small, xo, wo, so, sx, rx, sw, rw, sf, rf, sm, rm, ls):
    i, s = lax.axis_index("expert"), lax.axis_index("shard")
    core = lax.rem(i, 2)
    sib = i + 1 - 2 * core
    right, left, far = lax.rem(s + 1, NS), lax.rem(s + 3, NS), lax.rem(s + 2, NS)
    bar = pltpu.get_barrier_semaphore()
    for p in (right, left, far):
        pl.semaphore_signal(bar, inc=1, device_id=(i, p), device_id_type=MESH)
    pl.semaphore_signal(bar, inc=1, device_id=(sib, s), device_id_type=MESH)
    pl.semaphore_wait(bar, 4)

    def put(src, dst, a, b, dev):
        c = pltpu.make_async_remote_copy(src, dst, a, b, device_id=dev, device_id_type=MESH)
        c.start()
        return c

    top, bot = pl.ds(0, T // 2), pl.ds(T // 2, T // 2)
    sends = []
    for k, p in ((0, right), (1, left), (2, far)):
        sends.append(put(small, so.at[s], sm.at[k], rm.at[k], (i, p)))
    half = pl.ds(core * (T // 2), T // 2)
    for k, p in ((0, right), (1, left), (2, far)):
        sends.append(put(wq.at[half, pl.ds(p * 256, 256)], wo.at[s, half, pl.ds(0, 256)], sw.at[k, 0], rw.at[k, 0], (i, p)))
        sends.append(put(wk.at[half, pl.ds(p * 128, 128)], wo.at[s, half, pl.ds(256, 128)], sw.at[k, 1], rw.at[k, 1], (i, p)))
        sends.append(put(wv.at[half, pl.ds(p * 128, 128)], wo.at[s, half, pl.ds(384, 128)], sw.at[k, 2], rw.at[k, 2], (i, p)))
    rt = put(x.at[top], xo.at[s, top], sx.at[0], rx.at[0], (i, right))
    lb = put(x.at[bot], xo.at[s, bot], sx.at[1], rx.at[1], (i, left))
    rb = put(x.at[bot], xo.at[s, bot], sx.at[2], rx.at[2], (i, right))
    lt = put(x.at[top], xo.at[s, top], sx.at[3], rx.at[3], (i, left))
    loc = [
        pltpu.make_async_copy(x, xo.at[s], ls.at[0]),
        pltpu.make_async_copy(small, so.at[s], ls.at[1]),
        pltpu.make_async_copy(wq.at[:, pl.ds(s * 256, 256)], wo.at[s, :, pl.ds(0, 256)], ls.at[2]),
        pltpu.make_async_copy(wk.at[:, pl.ds(s * 128, 128)], wo.at[s, :, pl.ds(256, 128)], ls.at[3]),
        pltpu.make_async_copy(wv.at[:, pl.ds(s * 128, 128)], wo.at[s, :, pl.ds(384, 128)], ls.at[4]),
    ]
    for c in loc:
        c.start()
    for k, src in ((0, left), (1, right), (2, far)):
        for j in range(3):
            sends[3 + 3 * k + j].wait_recv()
        sends.append(put(wo.at[src, half], wo.at[src, half], sf.at[k], rf.at[k], (sib, s)))
    rt.wait_recv()
    ft = put(xo.at[left, top], xo.at[left, top], sx.at[4], rx.at[4], (i, right))
    lb.wait_recv()
    fb = put(xo.at[right, bot], xo.at[right, bot], sx.at[5], rx.at[5], (i, left))
    for c in (rb, lt, ft, fb):
        c.wait_recv()
    for c in sends[:3]:
        c.wait_recv()
    for c in sends[12:]:
        c.wait_recv()
    for c in sends + [rt, lb, rb, lt, ft, fb]:
        c.wait_send()
    for c in loc:
        c.wait()


def gather_front(x, wq, wk, wv, small):
    return pl.pallas_call(
        gather_front_kernel,
        out_shape=(sds((NS, T, D), BF), sds((NS, T, GC), BF), sds((NS,) + small.shape, F32)),
        in_specs=[ANY] * 5,
        out_specs=(ANY, ANY, ANY),
        scratch_shapes=[DMA((6,)), DMA((6,)), DMA((3, 3)), DMA((3, 3)), DMA((3,)), DMA((3,)), DMA((3,)), DMA((3,)), DMA((5,))],
        compiler_params=pltpu.CompilerParams(collective_id=0, has_side_effects=True),
        cost_estimate=pl.CostEstimate(flops=0, bytes_accessed=90 << 20, transcendentals=0),
        name="gather_front",
    )(x, wq, wk, wv, small)


def swap_kernel(x, o, ss, rs, ls):
    i, s = lax.axis_index("expert"), lax.axis_index("shard")
    peers = [lax.rem(s + k, NS) for k in (2, 1, 3)]
    bar = pltpu.get_barrier_semaphore()
    for p in peers:
        pl.semaphore_signal(bar, inc=1, device_id=(i, p), device_id_type=MESH)
    pl.semaphore_wait(bar, 3)
    copies = []
    for k, p in enumerate(peers):
        c = pltpu.make_async_remote_copy(x.at[p], o.at[s], ss.at[k], rs.at[k], device_id=(i, p), device_id_type=MESH)
        c.start()
        copies.append(c)
    loc = pltpu.make_async_copy(x.at[s], o.at[s], ls)
    loc.start()
    for c in copies:
        c.wait()
    loc.wait()


def swap(x, cid):
    return pl.pallas_call(
        swap_kernel,
        out_shape=sds(x.shape, x.dtype),
        in_specs=[ANY],
        out_specs=ANY,
        scratch_shapes=[DMA((3,)), DMA((3,)), DMA],
        compiler_params=pltpu.CompilerParams(collective_id=cid, has_side_effects=True),
        cost_estimate=pl.CostEstimate(flops=0, bytes_accessed=30 << 20, transcendentals=0),
        name="swap%d" % cid,
    )(x)


def reduce_kernel(
    a, b, g, ao, bo, go,
    pa, pb, pg, ya, yb, yg, a1, b1, g1, xa, xb, xg, a2, b2, g2, za, zb, zg, a3, b3, ra, rb, rg, og,
    ss, rs, ls,
):
    i, s = lax.axis_index("expert"), lax.axis_index("shard")
    core = lax.rem(i, 2)
    sib = i + 1 - 2 * core
    xi, zi = lax.rem(lax.div(i, 2), 4), lax.div(i, 8)

    def at_x(q):
        return (zi * 8 + q * 2 + core, s)

    def at_z(q):
        return (q * 8 + xi * 2 + core, s)

    bar = pltpu.get_barrier_semaphore()
    pl.semaphore_signal(bar, inc=1, device_id=(sib, s), device_id_type=MESH)
    for k in (1, 2, 3):
        pl.semaphore_signal(bar, inc=1, device_id=(i, lax.rem(s + k, 4)), device_id_type=MESH)
        pl.semaphore_signal(bar, inc=1, device_id=at_x(lax.rem(xi + k, 4)), device_id_type=MESH)
        pl.semaphore_signal(bar, inc=1, device_id=at_z(lax.rem(zi + k, 4)), device_id_type=MESH)
    pl.semaphore_wait(bar, 10)
    count = [0]

    def put(src, dst, dev):
        n = count[0]
        count[0] += 1
        c = pltpu.make_async_remote_copy(src, dst, ss.at[n], rs.at[n], device_id=dev, device_id_type=MESH)
        c.start()
        return c

    mine, other = core, 1 - core
    c0 = [
        put(a.at[:, pl.ds(other * 128, 128), :], pa, (sib, s)),
        put(b.at[:, pl.ds(other * 512, 512), :], pb, (sib, s)),
        put(g.at[:, :, pl.ds(other * 128, 128)], pg, (sib, s)),
    ]
    for c in c0:
        c.wait()
    for p in range(NS):
        ya[p] = (a[p, pl.ds(mine * 128, 128), :].astype(F32) + pa[p].astype(F32)).astype(BF)
        yb[p] = (b[p, pl.ds(mine * 512, 512), :].astype(F32) + pb[p].astype(F32)).astype(BF)
    yg[...] = g[:, :, pl.ds(mine * 128, 128)] + pg[...]
    c1 = []
    for k in (2, 1, 3):
        p = lax.rem(s + k, 4)
        c1.append(put(ya.at[p], a1.at[s], (i, p)))
        c1.append(put(yb.at[p], b1.at[k - 1], (i, p)))
        c1.append(put(yg.at[p], g1.at[k - 1], (i, p)))
    a1[s] = ya[s]
    for c in c1:
        c.wait()
    xb[...] = (yb[s].astype(F32) + b1[0].astype(F32) + b1[1].astype(F32) + b1[2].astype(F32)).astype(BF)
    xg[...] = yg[s] + g1[0] + g1[1] + g1[2]
    c2 = []
    for k in (2, 1, 3):
        q = lax.rem(xi + k, 4)
        c2.append(put(a1.at[q], a2.at[k - 1], at_x(q)))
        c2.append(put(xb.at[pl.ds(q * 128, 128), :], b2.at[k - 1], at_x(q)))
        c2.append(put(xg.at[pl.ds(q * 16, 16), :], g2.at[k - 1], at_x(q)))
    for c in c2:
        c.wait()
    za[...] = (a1[xi].astype(F32) + a2[0].astype(F32) + a2[1].astype(F32) + a2[2].astype(F32)).astype(BF)
    zb[...] = (
        xb[pl.ds(xi * 128, 128), :].astype(F32) + b2[0].astype(F32) + b2[1].astype(F32) + b2[2].astype(F32)
    ).astype(BF)
    zg[...] = xg[pl.ds(xi * 16, 16), :] + g2[0] + g2[1] + g2[2]
    c3 = []
    for k in (2, 1, 3):
        q = lax.rem(zi + k, 4)
        c3.append(put(za.at[pl.ds(q * 32, 32), :], a3.at[k - 1], at_z(q)))
        c3.append(put(zb.at[pl.ds(q * 32, 32), :], b3.at[k - 1], at_z(q)))
        c3.append(put(zg, rg.at[k - 1], at_z(q)))
    for c in c3:
        c.wait()
    own = pl.ds(zi * 32, 32)
    ra[xi, own, :] = (za[own, :].astype(F32) + a3[0].astype(F32) + a3[1].astype(F32) + a3[2].astype(F32)).astype(BF)
    rb[xi, own, :] = (zb[own, :].astype(F32) + b3[0].astype(F32) + b3[1].astype(F32) + b3[2].astype(F32)).astype(BF)
    og[pl.ds(xi * 16, 16), :] = zg[...] + rg[0] + rg[1] + rg[2]
    c4 = []
    for k in (2, 1, 3):
        q = lax.rem(zi + k, 4)
        c4.append(put(ra.at[xi, own, :], ra.at[xi, own, :], at_z(q)))
        c4.append(put(rb.at[xi, own, :], rb.at[xi, own, :], at_z(q)))
    for c in c4:
        c.wait()
    c5 = []
    for k in (2, 1, 3):
        q = lax.rem(xi + k, 4)
        c5.append(put(ra.at[xi], ra.at[xi], at_x(q)))
        c5.append(put(rb.at[xi], rb.at[xi], at_x(q)))
        c5.append(put(og.at[pl.ds(xi * 16, 16), :], og.at[pl.ds(xi * 16, 16), :], at_x(q)))
    for c in c5:
        c.wait()
    ha, hb, hg = pl.ds(core * 128, 128), pl.ds(core * 4, 4), pl.ds(core * 128, 128)
    c6 = [
        put(ra, ao.at[:, ha, :], (sib, s)),
        put(rb, bo.at[hb], (sib, s)),
        put(og, go.at[:, hg], (sib, s)),
    ]
    loc = [
        pltpu.make_async_copy(ra, ao.at[:, ha, :], ls.at[0]),
        pltpu.make_async_copy(rb, bo.at[hb], ls.at[1]),
        pltpu.make_async_copy(og, go.at[:, hg], ls.at[2]),
    ]
    for c in loc:
        c.start()
    for c in c6 + loc:
        c.wait()


def reduce_dense(a, b, g):
    v = pltpu.VMEM
    return pl.pallas_call(
        reduce_kernel,
        out_shape=(sds((NS, T, GC), BF), sds((8, 128, 256), BF), sds((SMALL, 256), F32)),
        in_specs=[VM, VM, VM],
        out_specs=(VM, VM, VM),
        scratch_shapes=[
            v((NS, 128, GC), BF), v((NS, 512, 256), BF), v((NS, SMALL, 128), F32),
            v((NS, 128, GC), BF), v((NS, 512, 256), BF), v((NS, SMALL, 128), F32),
            v((NS, 128, GC), BF), v((3, 512, 256), BF), v((3, SMALL, 128), F32),
            v((8, 128), BF), v((512, 256), BF), v((SMALL, 128), F32),
            v((3, 128, GC), BF), v((3, 128, 256), BF), v((3, 16, 128), F32),
            v((128, GC), BF), v((128, 256), BF), v((16, 128), F32),
            v((3, 32, GC), BF), v((3, 32, 256), BF),
            v((NS, 128, GC), BF), v((NS, 128, 256), BF), v((3, 16, 128), F32), v((SMALL, 128), F32),
            DMA((48,)), DMA((48,)), DMA((3,)),
        ],
        compiler_params=pltpu.CompilerParams(collective_id=4, has_side_effects=True, vmem_limit_bytes=48 << 20),
        cost_estimate=pl.CostEstimate(flops=0, bytes_accessed=150 << 20, transcendentals=0),
        name="reduce_dense",
    )(a, b, g)


def member_rank(ids):
    e = lax.broadcasted_iota(jnp.int32, (NE, T), 0)
    m = jnp.zeros((NE, T), F32)
    for k in range(TOPK):
        m = jnp.where(ids[k : k + 1, :] == e, 1.0, m)
    before = (lax.broadcasted_iota(jnp.int32, (T, T), 0) < lax.broadcasted_iota(jnp.int32, (T, T), 1)).astype(F32)
    rank = nn(m.astype(BF), before.astype(BF))
    return jnp.where(m > 0.5, rank, -1.0)


def onehot(rank_row, weight_row=None):
    c = lax.broadcasted_iota(jnp.int32, (CAP, T), 0).astype(F32)
    hit = c == rank_row
    return jnp.where(hit, 1.0 if weight_row is None else weight_row, 0.0)


def pack_cot_kernel(ids, cot, rank, out):
    r = member_rank(ids[...])
    rank[...] = r
    rows = cot[...]
    for q in range(NE // 4):
        p = jnp.concatenate([onehot(r[e : e + 1, :]) for e in range(4 * q, 4 * q + 4)], axis=0)
        out[q * 4 * CAP : (q + 1) * 4 * CAP, :] = nn(p.astype(BF), rows).astype(BF)


def rotate(v, cos, sin):
    lane = lax.broadcasted_iota(jnp.int32, v.shape, 1)
    partner = jnp.where(lax.rem(lane, 64) < 32, pltpu.roll(v, 96, 1), pltpu.roll(v, 32, 1))
    return v * cos + partner * sin


def allowed_block(seg_col, seg_row, qb, kb):
    same = seg_col[kb * T : (kb + 1) * T, :] == seg_row[:, qb * T : (qb + 1) * T]
    if qb == kb:
        same = same & (
            lax.broadcasted_iota(jnp.int32, (T, T), 0) <= lax.broadcasted_iota(jnp.int32, (T, T), 1)
        )
    m = same.astype(F32)
    return jnp.concatenate([m, m], axis=1) > 0.5


def attend_kernel(x, w, gain, cos, sin, seg_col, seg_row, att, attt, hid, q8, k, v, logt):
    wall = w[...].reshape(D, GC)
    for b in range(NS):
        xb = x[b].astype(F32)
        scale = lax.rsqrt(jnp.mean(xb * xb, axis=-1, keepdims=True) + EPS)
        h = (xb * scale * gain[...]).astype(BF)
        hid[b] = h
        qkv = nn(h, wall)
        rows = slice(b * T, (b + 1) * T)
        c, s = cos[rows, :], sin[rows, :]
        q0 = rotate(qkv[:, 0:128], c, s)
        q1 = rotate(qkv[:, 128:256], c, s)
        q8[rows, 0:128] = (q0 * HD**-0.5).astype(BF)
        q8[rows, 128:256] = (q1 * HD**-0.5).astype(BF)
        k[rows, :] = rotate(qkv[:, 256:384], c, s).astype(BF)
        v[rows, :] = qkv[:, 384:512].astype(BF)
    vt = [v[b * T : (b + 1) * T, :].astype(F32).T.astype(BF) for b in range(NS)]
    for qb in range(NS):
        rows = slice(qb * T, (qb + 1) * T)
        masks = [allowed_block(seg_col[...], seg_row[...], qb, kb) for kb in range(qb + 1)]
        parts = []
        for j in range(2):
            qs = jnp.concatenate([q8[rows, 128 * j : 128 * j + 64], q8[rows, 128 * j + 64 : 128 * j + 128]], axis=0)
            total = jnp.zeros((1, 2 * T), F32)
            ot = jnp.zeros((HD, 2 * T), F32)
            for kb in range(qb + 1):
                st = nt(k[kb * T : (kb + 1) * T, 64 * j : 64 * j + 64], qs)
                e = jnp.where(masks[kb], jnp.exp(st), 0.0)
                total = total + jnp.sum(e, axis=0, keepdims=True)
                ot = ot + nn(vt[kb][64 * j : 64 * j + 64, :], e.astype(BF))
            logt[qb * 2 + j : qb * 2 + j + 1, :] = jnp.log(total)
            ot = ot / total
            parts += [ot[:, :T], ot[:, T:]]
        at = jnp.concatenate(parts, axis=0)
        attt[qb] = at.astype(BF)
        att[qb] = at.T.astype(BF)


def attend_back_kernel(da, attt, hid, q8, k, v, logt, cos, sin, seg_col, seg_row, dqkv, gw, dk, dv):
    dk[...] = jnp.zeros_like(dk)
    dv[...] = jnp.zeros_like(dv)
    kt = [k[b * T : (b + 1) * T, :].astype(F32).T.astype(BF) for b in range(NS)]
    for qb in range(NS):
        rows = slice(qb * T, (qb + 1) * T)
        masks = [allowed_block(seg_col[...], seg_row[...], qb, kb) for kb in range(qb + 1)]
        dab = da[qb]
        prod = dab.astype(F32).T * attt[qb].astype(F32)
        parts = []
        for j in range(2):
            qs = jnp.concatenate([q8[rows, 128 * j : 128 * j + 64], q8[rows, 128 * j + 64 : 128 * j + 128]], axis=0)
            do = jnp.concatenate([dab[:, 128 * j : 128 * j + 64], dab[:, 128 * j + 64 : 128 * j + 128]], axis=0)
            delta = jnp.concatenate(
                [
                    jnp.sum(prod[128 * j : 128 * j + 64, :], axis=0, keepdims=True),
                    jnp.sum(prod[128 * j + 64 : 128 * j + 128, :], axis=0, keepdims=True),
                ],
                axis=1,
            )
            lt = logt[qb * 2 + j : qb * 2 + j + 1, :]
            dqt = jnp.zeros((HD, 2 * T), F32)
            for kb in range(qb + 1):
                keys = slice(kb * T, (kb + 1) * T)
                cols = slice(64 * j, 64 * j + 64)
                p = jnp.where(masks[kb], jnp.exp(nt(k[keys, cols], qs) - lt), 0.0)
                dv[keys, cols] += nn(p.astype(BF), do)
                dp = nt(v[keys, cols], do)
                ds = (p * (dp - delta)).astype(BF)
                dk[keys, cols] += nn(ds, qs)
                dqt = dqt + nn(kt[kb][cols, :], ds)
            dqt = dqt * HD**-0.5
            parts += [dqt[:, :T], dqt[:, T:]]
        dq = jnp.concatenate(parts, axis=0).T
        c, s = cos[rows, :], -sin[rows, :]
        dqkv[qb, :, 0:128] = rotate(dq[:, 0:128], c, s).astype(BF)
        dqkv[qb, :, 128:256] = rotate(dq[:, 128:256], c, s).astype(BF)
    for b in range(NS):
        rows = slice(b * T, (b + 1) * T)
        dqkv[b, :, 256:384] = rotate(dk[rows, :], cos[rows, :], -sin[rows, :]).astype(BF)
        dqkv[b, :, 384:512] = dv[rows, :].astype(BF)
    for r in range(NS):
        acc = jnp.zeros((T, GC), F32)
        for b in range(NS):
            acc = acc + tn(hid[b, :, r * T : (r + 1) * T], dqkv[b])
        gw[r] = acc.astype(BF)


def middle_kernel(att, x, wo, gain, router, rank, resid, hid, pgate, gates, out):
    cols = []
    for s in range(NS):
        acc = x[:, s * 256 : (s + 1) * 256].astype(F32)
        for g in range(NS):
            acc = acc + nn(att[g], wo[s, g * 256 : (g + 1) * 256, :])
        cols.append(acc)
    r = jnp.concatenate(cols, axis=1)
    resid[...] = r
    scale = lax.rsqrt(jnp.mean(r * r, axis=-1, keepdims=True) + EPS)
    h = (r * scale * gain[...]).astype(BF)
    hid[...] = h
    logits = nt(router[...].astype(BF), h)
    rk = rank[...]
    ex = jnp.where(rk >= 0.0, jnp.exp(logits), 0.0)
    gt = ex / jnp.sum(ex, axis=0, keepdims=True)
    gates[...] = gt
    for q in range(NE // 4):
        es = range(4 * q, 4 * q + 4)
        rows = slice(q * 4 * CAP, (q + 1) * 4 * CAP)
        p = jnp.concatenate([onehot(rk[e : e + 1, :]) for e in es], axis=0)
        out[rows, :] = nn(p.astype(BF), h).astype(BF)
        w = jnp.concatenate([onehot(rk[e : e + 1, :], gt[e : e + 1, :]) for e in es], axis=0)
        pgate[rows, :] = w.astype(BF)


def expert_kernel(h, cot, wg, wu, wd, drow, mid, dgp, dup, dg):
    hb = h[...]
    gp = nn(hb, wg[...])
    up = nn(hb, wu[...])
    dm = nt(cot[:, 0:256], wd[0])
    for s in range(1, NS):
        dm = dm + nt(cot[:, s * 256 : (s + 1) * 256], wd[s])
    sig = jax.nn.sigmoid(gp)
    act = gp * sig
    m = (act * up).astype(BF)
    mid[...] = m
    dg[...] = jnp.sum(dm * m.astype(F32), axis=1, keepdims=True)
    a = (dm * up * sig * (1.0 + gp * (1.0 - sig))).astype(BF)
    b = (dm * act).astype(BF)
    dgp[...] = a
    dup[...] = b
    drow[...] = (nt(a, wg[...]) + nt(b, wu[...])).astype(BF)


def experts(h, cot, wg, wu, wd):
    rows = 288
    full = lambda *sh: pl.BlockSpec(sh, lambda n: (0,) * len(sh), pipeline_mode=pl.Buffered(1))
    tile = lambda c: pl.BlockSpec((rows, c), lambda n: (n, 0))
    return pl.pallas_call(
        expert_kernel,
        grid=(SLOTS // rows,),
        out_shape=(sds((SLOTS, D), BF), sds((SLOTS, FF), BF), sds((SLOTS, FF), BF), sds((SLOTS, FF), BF), sds((SLOTS, 1), F32)),
        in_specs=[tile(D), tile(D), full(D, FF), full(D, FF), full(NS, FF, 256)],
        out_specs=(tile(D), tile(FF), tile(FF), tile(FF), tile(1)),
        compiler_params=pltpu.CompilerParams(vmem_limit_bytes=48 << 20),
        cost_estimate=pl.CostEstimate(flops=12 << 30, bytes_accessed=24 << 20, transcendentals=0),
        name="experts",
    )(h, cot, wg, wu, wd)


def middle_back_kernel(back, dgs, pgate, rank, gates, router, resid, gain, cot, wo, att, hid, dres, dat, gwo, small):
    rk, gt = rank[...], gates[...]
    dh = jnp.zeros((T, D), F32)
    rowsd = []
    for q in range(NE // 4):
        rows = slice(q * 4 * CAP, (q + 1) * 4 * CAP)
        dh = dh + tn(pgate[rows, :], back[rows, :])
        for e in range(4 * q, 4 * q + 4):
            rowsd.append(jnp.sum(onehot(rk[e : e + 1, :], dgs[:, e : e + 1]), axis=0, keepdims=True))
    dgate = jnp.concatenate(rowsd, axis=0)
    dch = gt * (dgate - jnp.sum(gt * dgate, axis=0, keepdims=True))
    dl = dch.astype(BF)
    small[0:NE, :] = nn(dl, hid[...])
    dh = dh + tn(dl, router[...].astype(BF))
    r = resid[...]
    scale = lax.rsqrt(jnp.mean(r * r, axis=-1, keepdims=True) + EPS)
    normed = r * scale
    small[NE : NE + 1, :] = jnp.sum(dh * normed, axis=0, keepdims=True)
    small[NE + 1 :, :] = jnp.zeros((SMALL - NE - 1, D), F32)
    m = dh * gain[...]
    dr = cot[...].astype(F32) + scale * (m - normed * jnp.mean(m * normed, axis=-1, keepdims=True))
    dres[...] = dr
    da = dr.astype(BF)
    for g in range(NS):
        acc = jnp.zeros((T, 256), F32)
        for s in range(NS):
            acc = acc + nt(da[:, s * 256 : (s + 1) * 256], wo[s, g * 256 : (g + 1) * 256, :])
        dat[g] = acc.astype(BF)
    for s in range(NS):
        for g in range(NS):
            gwo[s, g * 256 : (g + 1) * 256, :] = tn(att[g], da[:, s * 256 : (s + 1) * 256]).astype(BF)


def first_back_kernel(dqkv, wq, wk, wv, x, gain, dres, dtok, gnorm):
    dh = jnp.zeros((T, D), F32)
    for g in range(NS):
        dh = dh + nt(dqkv[g, :, 0:256], wq[:, g * 256 : (g + 1) * 256])
        dh = dh + nt(dqkv[g, :, 256:384], wk[:, g * 128 : (g + 1) * 128])
        dh = dh + nt(dqkv[g, :, 384:512], wv[:, g * 128 : (g + 1) * 128])
    xf = x[...].astype(F32)
    scale = lax.rsqrt(jnp.mean(xf * xf, axis=-1, keepdims=True) + EPS)
    normed = xf * scale
    gnorm[...] = jnp.broadcast_to(jnp.sum(dh * normed, axis=0, keepdims=True), (8, D))
    n = dh * gain[...]
    dtok[...] = (dres[...] + scale * (n - normed * jnp.mean(n * normed, axis=-1, keepdims=True))).astype(BF)


def per_device(
    tokens, segments, expert_ids, attn_norm, query_weight, key_matrix, value_matrix, output_weight,
    ffn_norm, router_weight, gate_weight, up_weight, down_weight, cotangent,
):
    a2a = lambda v: lax.all_to_all(v, "expert", split_axis=0, concat_axis=0, tiled=True)
    gather = lambda v, axis: lax.all_gather(v, "shard", axis=axis, tiled=True)
    stack = lambda v: lax.all_gather(v, "shard", axis=0, tiled=False)

    rank, cot_rows = plain(
        pack_cot_kernel, (sds((NE, T), F32), sds((SLOTS, D), BF)), expert_ids.T, cotangent,
        name="pack_cot", flops=2 << 30, moved=6 << 20,
    )
    cot_recv = a2a(cot_rows.reshape(NE, CAP, D)).reshape(SLOTS, D)

    small = jnp.concatenate(
        [
            router_weight.T.astype(F32),
            attn_norm.astype(F32)[None],
            ffn_norm.astype(F32)[None],
            segments.astype(F32),
            jnp.zeros((5, T), F32),
        ],
        axis=0,
    )
    x_all, w_group, small_all = gather_front(tokens, query_weight, key_matrix, value_matrix, small)
    small_full = small_all.transpose(1, 0, 2).reshape(40, D)
    router, gain_one, gain_two, seg_row = small_full[:NE], small_full[32:33], small_full[33:34], small_full[34:35]
    seg_col = seg_row.reshape(D, 1)

    wo = stack(output_weight)
    wg = gather(gate_weight[0], 0)
    wu = gather(up_weight[0], 0)
    wd = stack(down_weight[0])
    wq = gather(query_weight, 0)
    wk = gather(key_matrix, 0)
    wv = gather(value_matrix, 0)

    inverse = BASE ** (-jnp.arange(HD // 2, dtype=F32) * 2.0 / HD)
    angles = jnp.arange(D, dtype=F32)[:, None] * inverse[None, :]
    co, si = jnp.cos(angles), jnp.sin(angles)
    cos = jnp.concatenate([co, co, co, co], axis=1)
    sin = jnp.concatenate([-si, si, -si, si], axis=1)

    att, attt, hid_one, q8, k, v, logt = plain(
        attend_kernel,
        (
            sds((NS, T, 256), BF), sds((NS, 256, T), BF), sds((NS, T, D), BF), sds((D, 256), BF),
            sds((D, 128), BF), sds((D, 128), BF), sds((8, 512), F32),
        ),
        x_all, w_group, gain_one, cos, sin, seg_col, seg_row,
        name="attend", flops=2 << 30, moved=10 << 20,
    )
    att_rows = swap(att, 1)
    resid, hid_two, pgate, gates, send = plain(
        middle_kernel,
        (sds((T, D), F32), sds((T, D), BF), sds((SLOTS, T), BF), sds((NE, T), F32), sds((SLOTS, D), BF)),
        att_rows, tokens, wo, gain_two, router, rank,
        name="middle", flops=2 << 30, moved=10 << 20,
    )
    recv = a2a(send.reshape(NE, CAP, D)).reshape(SLOTS, D)
    hit = rank[:, None, :] == jnp.arange(CAP, dtype=F32)[None, :, None]
    gate_slots = jnp.sum(jnp.where(hit, gates[:, None, :], 0.0), axis=2)
    gate_recv = a2a(gate_slots).reshape(SLOTS, 1)

    drow, mid, dgp, dup, dg = experts(recv, cot_recv, wg, wu, wd)
    back = a2a(drow.reshape(NE, CAP, D)).reshape(SLOTS, D)
    dgs = a2a(dg.reshape(NE, CAP)).T

    wd_rows = wd.transpose(1, 0, 2).reshape(FF, D)
    out_rows = jnp.dot(mid, wd_rows, preferred_element_type=F32).astype(BF)
    out_back = a2a(out_rows.reshape(NE, CAP, D)).reshape(SLOTS, D)
    scaled = lambda u: (u.astype(F32) * gate_recv).astype(BF)
    grad_down = jnp.einsum("nf,nd->fd", mid, scaled(cot_recv), preferred_element_type=F32)
    grad_gate = jnp.einsum("nd,nf->df", recv, scaled(dgp), preferred_element_type=F32)
    grad_up = jnp.einsum("nd,nf->df", recv, scaled(dup), preferred_element_type=F32)
    scatter = lambda u, d: lax.psum_scatter(u[None].astype(BF), "shard", scatter_dimension=d, tiled=True).astype(F32)
    d_gate, d_up, d_down = scatter(grad_gate, 1), scatter(grad_up, 1), scatter(grad_down, 2)

    combined = jnp.einsum("nt,nd->td", pgate, out_back, preferred_element_type=F32)
    output = (resid + combined).astype(BF)

    dres, dat, gwo, small_grad = plain(
        middle_back_kernel,
        (sds((T, D), F32), sds((NS, T, 256), BF), sds((NS, D, 256), BF), sds((SMALL, D), F32)),
        back, dgs, pgate, rank, gates, router, resid, gain_two, cotangent, wo, att_rows, hid_two,
        name="middle_back", flops=4 << 30, moved=14 << 20,
    )
    dat_seq = swap(dat, 2)
    dqkv, gw = plain(
        attend_back_kernel,
        (sds((NS, T, GC), BF), sds((NS, T, GC), BF)),
        dat_seq, attt, hid_one, q8, k, v, logt, cos, sin, seg_col, seg_row,
        name="attend_back", flops=4 << 30, moved=10 << 20,
        scratch_shapes=[pltpu.VMEM((D, 128), F32), pltpu.VMEM((D, 128), F32)],
    )
    dqkv_rows = swap(dqkv, 3)
    d_tokens, gnorm = plain(
        first_back_kernel,
        (sds((T, D), BF), sds((8, D), F32)),
        dqkv_rows, wq, wk, wv, tokens, gain_one, dres,
        name="first_back", flops=1 << 30, moved=8 << 20,
    )
    small_sum = jnp.concatenate([small_grad[: NE + 1], gnorm[:1], small_grad[NE + 2 :]], axis=0)
    ga, gb, gs = reduce_dense(gw, gwo, small_sum.reshape(SMALL, NS, T).transpose(1, 0, 2))
    ga, gb = ga.astype(F32), gb.astype(F32)
    d_query = ga[:, :, 0:256].transpose(1, 0, 2).reshape(T, D)
    d_key = ga[:, :, 256:384].transpose(1, 0, 2).reshape(T, 512)
    d_value = ga[:, :, 384:512].transpose(1, 0, 2).reshape(T, 512)
    d_output_weight = gb.reshape(D, 256)
    d_router, d_ffn_norm, d_attn_norm = gs[:NE].T, gs[NE], gs[NE + 1]
    return (
        output, d_tokens, d_attn_norm, d_query, d_key, d_value, d_output_weight, d_ffn_norm, d_router,
        d_gate, d_up, d_down,
    )


def solution(mesh):
    rows = P(("expert", "shard"), None)
    return jax.shard_map(
        per_device,
        mesh=mesh,
        in_specs=(
            rows, P("expert", "shard"), rows, P("shard"), P("shard", None), P("shard", None), P("shard", None),
            P(None, "shard"), P("shard"), P("shard", None), P("expert", "shard", None), P("expert", "shard", None),
            P("expert", None, "shard"), rows,
        ),
        out_specs=(
            rows, rows, P("shard"), P("shard", None), P("shard", None), P("shard", None), P(None, "shard"),
            P("shard"), P("shard", None), P("expert", "shard", None), P("expert", "shard", None),
            P("expert", None, "shard"),
        ),
        check_vma=False,
    )
```
